32 devices in a mesh: groups: 2 (over y), blk: 4 (over z), head: 2 (over x), rep: 2 (over core).
Axes of the slice: x: 2, y: 2, z: 4, core: 2. Of those that a mesh axis runs over, the one named last changes fastest.
Arguments:
- queries: bfloat16 [4, 4096, 1024], P('groups', ('blk', 'rep'), 'head'), parts along dimension 0, may hold values from -24 to 24
- prefix_keys: bfloat16 [4, 8192, 128], P('groups', ('blk', 'head')), parts along dimension 0, may hold values from -6 to 6
- prefix_values: bfloat16 [4, 8192, 128], P('groups', ('blk', 'head')), parts along dimension 0, may hold values from -6 to 6
- stretch_keys: bfloat16 [4, 4096, 128], P('groups', ('blk', 'head')), parts along dimension 0, may hold values from -6 to 6
- stretch_values: bfloat16 [4, 4096, 128], P('groups', ('blk', 'head')), parts along dimension 0, may hold values from -6 to 6
- prefix_lengths: int32 [4], P('groups'), parts along dimension 0, may hold values from 128 to 8192, as said below
- decode_queries: bfloat16 [8, 64, 1024], P('groups', 'rep'), parts along dimension 0, may hold values from -24 to 24
- new_keys: bfloat16 [8, 64, 128], P('groups', 'rep'), parts along dimension 0, may hold values from -6 to 6
- new_values: bfloat16 [8, 64, 128], P('groups', 'rep'), parts along dimension 0, may hold values from -6 to 6
- row_prompts: int32 [128], P(('groups', 'rep')), parts along dimension 0, may hold values from 0 to 1
Outputs:
- prefill_out: bfloat16 [4, 4096, 1024], P('groups', ('blk', 'rep'), 'head'), parts along dimension 0
- decode_out: bfloat16 [8, 64, 1024], P('groups', 'rep'), parts along dimension 0
The draws below stay inside these ranges and needn't reach their ends.
There are 2 independent parts, one for each index of `groups`. The reference program is written for one: setup_inputs(seed, part) draws one part's arguments, and reference() takes and returns one part's arrays. A program takes and returns all parts, laid end to end along the dimension named above; each array names one. Nothing has to cross between parts.
Inputs may be any that keep to these rules, and one draw needn't show every extreme that they name: `prefix_lengths`: multiples of 128; in every draw some prompt has exactly 8192.
All inputs are finite; a program needn't handle non-finite values.
Results may differ from the reference program's by a relative error of at most 0.0095.
Values may be sent and summed in bfloat16 or wider, within the bound.
A program may use at most 192 MiB of HBM per device.

```python
import jax
import jax.numpy as jnp
from jax import lax

HEADS = 8
HEAD_DIM = 128
PREFIX = 8192
STRETCH = 4096
STEPS = 4
ROWS = 64
PROMPTS = 2


def drawn_keys(key, salt, shape):
    subkey = jax.random.fold_in(key, salt)
    values = jnp.clip(jax.random.normal(subkey, shape, jnp.float32), -6.0, 6.0)
    return values.astype(jnp.bfloat16)


def drawn_queries(key, salt, shape):
    subkey = jax.random.fold_in(key, salt)
    values = jnp.clip(jax.random.normal(subkey, shape, jnp.float32), -6.0, 6.0)
    return values.astype(jnp.bfloat16)


def draw_queries(key, part):
    return drawn_queries(key, 11, (PROMPTS, STRETCH, HEADS * HEAD_DIM))


def draw_prefix_keys(key, part):
    return drawn_keys(key, 12, (PROMPTS, PREFIX, HEAD_DIM))


def draw_stretch_keys(key, part):
    return drawn_keys(key, 13, (PROMPTS, STRETCH, HEAD_DIM))


def draw_decode_queries(key, part):
    return drawn_queries(key, 14, (STEPS, ROWS, HEADS * HEAD_DIM))


def draw_new_keys(key, part):
    return drawn_keys(key, 15, (STEPS, ROWS, HEAD_DIM))


def draw_prefix_lengths(key, part):
    whole_units = PREFIX // 128
    units = jax.random.randint(jax.random.fold_in(key, 16), (PROMPTS,), 1, whole_units + 1)
    fullest = jax.random.randint(jax.random.fold_in(key, 17), (), 0, PROMPTS)
    units = jnp.where(jnp.arange(PROMPTS, dtype=jnp.int32) == fullest, whole_units, units)
    return (units * 128).astype(jnp.int32)


def plant(values, rng, low, high):
    shape = values.shape
    place = [jax.random.randint(jax.random.fold_in(rng, axis), (), 0, shape[axis]) for axis in range(len(shape))]
    values = values.at[tuple(place)].set(low)
    longest = shape.index(max(shape))
    place[longest] = (place[longest] + 1) % shape[longest]
    return values.at[tuple(place)].set(high)


def block_levels(own_key, shape, cuts, low, largest):
    def one(dim, parts):
        steps = jax.random.uniform(jax.random.fold_in(jax.random.fold_in(own_key, 6), dim), (parts,), jnp.float32, low / len(cuts), largest / len(cuts))
        return jnp.repeat(jnp.exp(steps), shape[dim] // parts).reshape((-1,) + (1,) * (len(shape) - dim - 1))

    loudness = one(*cuts[0])
    for cut in cuts[1:]:
        loudness = loudness * one(*cut)
    return loudness


def noise(rng, dims, spread, reach, cuts=(), kind=jnp.bfloat16):
    loudness = block_levels(rng, dims, cuts, -0.22, 0.18) if cuts else 1.0
    values = jax.random.normal(rng, dims, jnp.float32) * spread * loudness
    return jnp.minimum(jnp.maximum(values, -reach), reach).astype(kind)


def setup_inputs(seed: int = 0, part: int = 0) -> dict:
    key_of = jax.random.split(jax.random.key(seed), 11)
    part_keys = jax.random.split(jax.random.fold_in(key_of[10], part), 11)
    queries = draw_queries(jax.random.fold_in(jax.random.fold_in(key_of[10], part), 71), part)
    prefix_keys = draw_prefix_keys(jax.random.fold_in(jax.random.fold_in(key_of[10], part), 71), part)
    prefix_values = noise(part_keys[2], (PROMPTS, PREFIX, HEAD_DIM), 1.0, 6.0, ((1, 8),))
    stretch_keys = draw_stretch_keys(jax.random.fold_in(jax.random.fold_in(key_of[10], part), 71), part)
    stretch_values = noise(part_keys[4], (PROMPTS, STRETCH, HEAD_DIM), 1.0, 6.0, ((1, 8),))
    prefix_lengths = draw_prefix_lengths(jax.random.fold_in(jax.random.fold_in(key_of[10], part), 71), part)
    decode_queries = draw_decode_queries(jax.random.fold_in(jax.random.fold_in(key_of[10], part), 71), part)
    new_keys = draw_new_keys(jax.random.fold_in(jax.random.fold_in(key_of[10], part), 71), part)
    new_values = noise(part_keys[8], (STEPS, ROWS, HEAD_DIM), 1.0, 6.0, ((1, 2),))
    row_prompts = plant(jax.random.randint(part_keys[9], (ROWS,), 0, PROMPTS), jax.random.fold_in(part_keys[9], 1), 0, PROMPTS - 1).astype(jnp.int32)
    return {"queries": queries, "prefix_keys": prefix_keys, "prefix_values": prefix_values, "stretch_keys": stretch_keys, "stretch_values": stretch_values, "prefix_lengths": prefix_lengths, "decode_queries": decode_queries, "new_keys": new_keys, "new_values": new_values, "row_prompts": row_prompts}


def soft_weights(score_list, mask_list):
    maxima = None
    for scores, visible in zip(score_list, mask_list):
        local_max = jnp.max(jnp.where(visible, scores, -jnp.inf), axis=-1)
        maxima = local_max if maxima is None else jnp.maximum(maxima, local_max)
    weight_list = []
    denominator = None
    for scores, visible in zip(score_list, mask_list):
        weight = jnp.where(visible, jnp.exp(scores - maxima[..., None]), jnp.float32(0.0))
        partial_sum = jnp.sum(weight, axis=-1)
        denominator = partial_sum if denominator is None else denominator + partial_sum
        weight_list.append(weight.astype(jnp.bfloat16))
    return weight_list, denominator


def reference(queries, prefix_keys, prefix_values, stretch_keys, stretch_values, prefix_lengths, decode_queries, new_keys, new_values, row_prompts):
    scaling = HEAD_DIM ** -0.5
    block_len = min(512, STRETCH)

    def one_prompt(inputs):
        prompt_q, pre_k, pre_v, chk_k, chk_v, length = inputs

        def one_block(block_index):
            first_row = (block_index * block_len).astype(jnp.int32)
            query_rows = lax.dynamic_slice_in_dim(prompt_q, first_row, block_len, 0)
            query_rows = query_rows.reshape(block_len, HEADS, HEAD_DIM).astype(jnp.float32)
            pre_scores = jnp.einsum('qhd,kd->qhk', query_rows, pre_k.astype(jnp.float32)) * scaling
            chk_scores = jnp.einsum('qhd,kd->qhk', query_rows, chk_k.astype(jnp.float32)) * scaling
            query_pos = first_row + jnp.arange(block_len, dtype=jnp.int32)
            pre_seen = (jnp.arange(PREFIX, dtype=jnp.int32) < length)[None, None, :]
            chk_seen = (jnp.arange(STRETCH, dtype=jnp.int32)[None, :] <= query_pos[:, None])[:, None, :]
            weight_list, denominator = soft_weights([pre_scores, chk_scores], [pre_seen, chk_seen])
            weighted = jnp.einsum('qhk,kd->qhd', weight_list[0].astype(jnp.float32), pre_v.astype(jnp.float32))
            weighted = weighted + jnp.einsum('qhk,kd->qhd', weight_list[1].astype(jnp.float32), chk_v.astype(jnp.float32))
            result = (weighted / denominator[..., None]).astype(jnp.bfloat16)
            return result.reshape(block_len, HEADS * HEAD_DIM)

        blocks = lax.map(one_block, jnp.arange(STRETCH // block_len, dtype=jnp.int32))
        return blocks.reshape(STRETCH, HEADS * HEAD_DIM)

    prefill_out = lax.map(one_prompt, (queries, prefix_keys, prefix_values, stretch_keys, stretch_values, prefix_lengths))

    decode_rows = decode_queries.reshape(STEPS, ROWS, HEADS, HEAD_DIM).astype(jnp.float32)
    row_pre_k = prefix_keys[row_prompts].astype(jnp.float32)
    row_pre_v = prefix_values[row_prompts].astype(jnp.float32)
    row_chk_k = stretch_keys[row_prompts].astype(jnp.float32)
    row_chk_v = stretch_values[row_prompts].astype(jnp.float32)
    pre_scores = jnp.einsum('srhd,rkd->srhk', decode_rows, row_pre_k) * scaling
    chk_scores = jnp.einsum('srhd,rkd->srhk', decode_rows, row_chk_k) * scaling
    own_scores = jnp.einsum('srhd,trd->srht', decode_rows, new_keys.astype(jnp.float32)) * scaling
    row_lengths = prefix_lengths[row_prompts]
    pre_seen = (jnp.arange(PREFIX, dtype=jnp.int32)[None, :] < row_lengths[:, None])[None, :, None, :]
    chk_seen = jnp.ones((1, 1, 1, STRETCH), dtype=bool)
    step_ids = jnp.arange(STEPS, dtype=jnp.int32)
    own_seen = (step_ids[None, :] <= step_ids[:, None])[:, None, None, :]
    weight_list, denominator = soft_weights([pre_scores, chk_scores, own_scores], [pre_seen, chk_seen, own_seen])
    weighted = jnp.einsum('srhk,rkd->srhd', weight_list[0].astype(jnp.float32), row_pre_v)
    weighted = weighted + jnp.einsum('srhk,rkd->srhd', weight_list[1].astype(jnp.float32), row_chk_v)
    weighted = weighted + jnp.einsum('srht,trd->srhd', weight_list[2].astype(jnp.float32), new_values.astype(jnp.float32))
    decode_out = (weighted / denominator[..., None]).astype(jnp.bfloat16).reshape(STEPS, ROWS, HEADS * HEAD_DIM)
    return prefill_out, decode_out
```

```python
import functools

import jax
import jax.numpy as jnp
from jax import lax
from jax.experimental import pallas as pl
from jax.experimental.pallas import tpu as pltpu
from jax.sharding import PartitionSpec as P

HEAD_DIM = 128
SCALE_LOG2E = HEAD_DIM ** (-0.5) * 1.4426950408889634
LOW = -1e30


def fold(q, k, v, m_ref, acc_ref, bias=None):
    s = lax.dot_general(q, k, (((1,), (1,)), ((), ())), preferred_element_type=jnp.float32)
    if bias is not None:
        s = jnp.where(bias, s, LOW)
    m_prev = m_ref[...]
    m_new = jnp.maximum(m_prev, jnp.max(s, axis=-1, keepdims=True))
    p = jnp.exp2(s * SCALE_LOG2E - (m_new * SCALE_LOG2E)[:, :1]).astype(jnp.bfloat16)
    alpha = jnp.exp2((m_prev - m_new) * SCALE_LOG2E)
    alpha2 = jnp.concatenate([alpha, alpha], axis=1)
    pv = jnp.dot(p, v, preferred_element_type=jnp.float32)
    acc_ref[...] = acc_ref[...] * alpha2 + pv
    m_ref[...] = m_new


def start_state(m_ref, acc_ref):
    m_ref[...] = jnp.full_like(m_ref, LOW)
    acc_ref[...] = jnp.zeros_like(acc_ref)


def fold_prefix(q, k_ref, v2_ref, length, block, m_ref, acc_ref):
    full = length // block

    @pl.loop(0, full)
    def _(i):
        rows = pl.ds(pl.multiple_of(i * block, block), block)
        fold(q, k_ref[rows, :], v2_ref[rows, :], m_ref, acc_ref)

    @pl.when(full * block < length)
    def _():
        rows = pl.ds(pl.multiple_of(full * block, block), block)
        spot = full * block + lax.broadcasted_iota(jnp.int32, (q.shape[0], block), 1)
        fold(q, k_ref[rows, :], v2_ref[rows, :], m_ref, acc_ref, spot < length)


def finish(acc_ref):
    return (acc_ref[:, :HEAD_DIM] / acc_ref[:, HEAD_DIM:]).astype(jnp.bfloat16)


def prefill_kernel(block, info, q_ref, pre_ref, chk_ref, o_ref, pv2, cv2, m_ref, acc_ref):
    q_rows = q_ref.shape[1]

    @pl.when(pl.program_id(0) == 0)
    def _():
        pv2[:, :HEAD_DIM] = pre_ref[1]
        pv2[:, HEAD_DIM:] = jnp.ones((pv2.shape[0], HEAD_DIM), jnp.bfloat16)
        cv2[:, :HEAD_DIM] = chk_ref[1]
        cv2[:, HEAD_DIM:] = jnp.ones((cv2.shape[0], HEAD_DIM), jnp.bfloat16)

    q = q_ref[0]
    start_state(m_ref, acc_ref)
    here = info[1]
    rows = pl.ds(pl.multiple_of(here * q_rows, q_rows), q_rows)
    seen = lax.broadcasted_iota(jnp.int32, (q_rows, q_rows), 1) <= lax.broadcasted_iota(
        jnp.int32, (q_rows, q_rows), 0
    )
    fold(q, chk_ref[0, rows, :], cv2[rows, :], m_ref, acc_ref, seen)

    @pl.loop(0, here)
    def _(i):
        rows = pl.ds(pl.multiple_of(i * q_rows, q_rows), q_rows)
        fold(q, chk_ref[0, rows, :], cv2[rows, :], m_ref, acc_ref)

    fold_prefix(q, pre_ref.at[0], pv2, info[0], block, m_ref, acc_ref)
    o_ref[0] = finish(acc_ref)


def decode_kernel(
    block, heads, row_dev, info, q_ref, nk_ref, nv_ref, pre_ref, chk_ref, o_ref, pv2, cv2, nv2, m_ref, acc_ref
):
    pv2[:, :HEAD_DIM] = pre_ref[1]
    pv2[:, HEAD_DIM:] = jnp.ones((pv2.shape[0], HEAD_DIM), jnp.bfloat16)
    cv2[:, :HEAD_DIM] = chk_ref[1]
    cv2[:, HEAD_DIM:] = jnp.ones((cv2.shape[0], HEAD_DIM), jnp.bfloat16)
    nv2[:, :HEAD_DIM] = nv_ref[...]
    nv2[:, HEAD_DIM:] = jnp.ones((nv2.shape[0], HEAD_DIM), jnp.bfloat16)
    q = q_ref[...]
    start_state(m_ref, acc_ref)
    count = q.shape[0]
    fresh = nk_ref.shape[0]
    row = info[1] * count + lax.broadcasted_iota(jnp.int32, (count, fresh), 0)
    col = lax.broadcasted_iota(jnp.int32, (count, fresh), 1)
    own = ((row // heads) % row_dev == col % row_dev) & (col // row_dev <= row // (heads * row_dev))
    fold(q, nk_ref[...], nv2[...], m_ref, acc_ref, own)

    @pl.loop(0, chk_ref.shape[1] // block)
    def _(i):
        rows = pl.ds(pl.multiple_of(i * block, block), block)
        fold(q, chk_ref[0, rows, :], cv2[rows, :], m_ref, acc_ref)

    fold_prefix(q, pre_ref.at[0], pv2, info[0], block, m_ref, acc_ref)
    o_ref[...] = finish(acc_ref)


def prefill(info, q, pre, chk, block):
    _, q_rows, width = q.shape
    heads = width // HEAD_DIM
    return pl.pallas_call(
        functools.partial(prefill_kernel, block),
        out_shape=jax.ShapeDtypeStruct(q.shape, jnp.bfloat16),
        grid_spec=pltpu.PrefetchScalarGridSpec(
            num_scalar_prefetch=1,
            grid=(heads,),
            in_specs=[
                pl.BlockSpec((1, q_rows, HEAD_DIM), lambda h, info: (0, 0, h)),
                pl.BlockSpec(pre.shape, lambda h, info: (0, 0, 0), pipeline_mode=pl.Buffered(1)),
                pl.BlockSpec(chk.shape, lambda h, info: (0, 0, 0), pipeline_mode=pl.Buffered(1)),
            ],
            out_specs=pl.BlockSpec((1, q_rows, HEAD_DIM), lambda h, info: (0, 0, h)),
            scratch_shapes=[
                pltpu.VMEM((pre.shape[1], 2 * HEAD_DIM), jnp.bfloat16),
                pltpu.VMEM((chk.shape[1], 2 * HEAD_DIM), jnp.bfloat16),
                pltpu.VMEM((q_rows, HEAD_DIM), jnp.float32),
                pltpu.VMEM((q_rows, 2 * HEAD_DIM), jnp.float32),
            ],
        ),
        compiler_params=pltpu.CompilerParams(
            dimension_semantics=("arbitrary",), vmem_limit_bytes=56 * 2**20
        ),
        name="prefill",
    )(info, q, pre, chk)


def decode(info, q, nk, nv, pre, chk, block, heads, row_dev):
    whole = pl.BlockSpec(memory_space=pltpu.VMEM)
    return pl.pallas_call(
        functools.partial(decode_kernel, block, heads, row_dev),
        out_shape=jax.ShapeDtypeStruct(q.shape, jnp.bfloat16),
        in_specs=[pl.BlockSpec(memory_space=pltpu.SMEM)] + [whole] * 5,
        out_specs=whole,
        scratch_shapes=[
            pltpu.VMEM((pre.shape[1], 2 * HEAD_DIM), jnp.bfloat16),
            pltpu.VMEM((chk.shape[1], 2 * HEAD_DIM), jnp.bfloat16),
            pltpu.VMEM((nk.shape[0], 2 * HEAD_DIM), jnp.bfloat16),
            pltpu.VMEM((q.shape[0], HEAD_DIM), jnp.float32),
            pltpu.VMEM((q.shape[0], 2 * HEAD_DIM), jnp.float32),
        ],
        compiler_params=pltpu.CompilerParams(vmem_limit_bytes=56 * 2**20),
        name="decode",
    )(info, q, nk, nv, pre, chk)


def local(
    queries,
    prefix_keys,
    prefix_values,
    stretch_keys,
    stretch_values,
    prefix_lengths,
    decode_queries,
    new_keys,
    new_values,
    row_prompts,
):
    prompts, q_rows, width = queries.shape
    heads_axis, blk_axis = lax.axis_size("head"), lax.axis_size("blk")
    assert prompts == heads_axis and lax.axis_size("rep") == 2
    side = lax.axis_index("rep") == 0
    pre = jnp.where(side, prefix_keys, prefix_values)
    chk = jnp.where(side, stretch_keys, stretch_values)
    pre_rows = pre.shape[1]
    both = jnp.concatenate([pre, chk], axis=1)
    moved = lax.all_to_all(both, "head", split_axis=0, concat_axis=0, tiled=True)
    gathered = lax.all_gather(moved, "blk", axis=0, tiled=True)
    gathered = lax.all_gather(gathered, "rep", axis=0)
    pre_all = gathered[:, :, :pre_rows].reshape(2, -1, HEAD_DIM)
    chk_all = gathered[:, :, pre_rows:].reshape(2, -1, HEAD_DIM)
    mine = lax.all_to_all(queries, "head", split_axis=0, concat_axis=2, tiled=True)
    length = lax.dynamic_index_in_dim(prefix_lengths, lax.axis_index("head"), keepdims=False)
    block = 1024

    steps, row_dev, decode_width = decode_queries.shape
    heads_all = decode_width // HEAD_DIM
    rows_all = steps * row_dev * heads_all
    share = rows_all // blk_axis
    dq = lax.dynamic_slice_in_dim(
        decode_queries.reshape(rows_all, HEAD_DIM), lax.axis_index("blk") * share, share, 0
    )
    dec = decode(
        jnp.stack([length, lax.axis_index("blk")]).astype(jnp.int32),
        dq,
        new_keys.reshape(-1, HEAD_DIM),
        new_values.reshape(-1, HEAD_DIM),
        pre_all,
        chk_all,
        block,
        heads_all,
        row_dev,
    )
    dec_all = lax.all_gather(dec, ("head", "blk"), axis=0, tiled=True)
    dec_all = dec_all.reshape(heads_axis, steps, row_dev, decode_width)
    decode_out = dec_all[0]
    for index in range(1, heads_axis):
        decode_out = jnp.where((row_prompts == index)[None, :, None], dec_all[index], decode_out)

    out = prefill(
        jnp.stack([length, lax.axis_index(("blk", "rep"))]).astype(jnp.int32), mine, pre_all, chk_all, block
    )
    prefill_out = lax.all_to_all(out, "head", split_axis=2, concat_axis=0, tiled=True)
    return (prefill_out, decode_out)


def solution(mesh):
    placed = (
        P("groups", ("blk", "rep"), "head"),
        P("groups", ("blk", "head"), None),
        P("groups", ("blk", "head"), None),
        P("groups", ("blk", "head"), None),
        P("groups", ("blk", "head"), None),
        P("groups"),
        P("groups", "rep", None),
        P("groups", "rep", None),
        P("groups", "rep", None),
        P(("groups", "rep")),
    )
    return jax.shard_map(
        local,
        mesh=mesh,
        in_specs=placed,
        out_specs=(P("groups", ("blk", "rep"), "head"), P("groups", "rep", None)),
        check_vma=False,
    )
```

```python
import functools

import jax
import jax.numpy as jnp
from jax import lax
from jax.experimental import pallas as pl
from jax.experimental.pallas import tpu as pltpu
from jax.sharding import PartitionSpec as P

HEAD_DIM = 128
SCALE_LOG2E = HEAD_DIM ** (-0.5) * 1.4426950408889634
LOW = -1e30
CHAIN = 128


def fold(q_of, rows, k, v2, m_ref, acc_ref, seen=None):
    chain = min(CHAIN, rows)
    scores = []
    for start in range(0, rows, chain):
        s = lax.dot_general(
            q_of(start, chain), k, (((1,), (1,)), ((), ())), preferred_element_type=jnp.float32
        )
        if seen is not None:
            s = jnp.where(seen(start, s.shape), s, LOW)
        scores.append(s)
    for index, start in enumerate(range(0, rows, chain)):
        s = scores[index]
        here = pl.ds(start, chain)
        m_prev = m_ref[here, :]
        m_new = jnp.maximum(m_prev, jnp.max(s, axis=-1, keepdims=True))
        p = jnp.exp2(s * SCALE_LOG2E - (m_new * SCALE_LOG2E)[:, :1]).astype(jnp.bfloat16)
        alpha = jnp.exp2((m_prev - m_new) * SCALE_LOG2E)
        alpha2 = jnp.concatenate([alpha, alpha], axis=1)
        acc_ref[here, :] = acc_ref[here, :] * alpha2 + jnp.dot(
            p, v2, preferred_element_type=jnp.float32
        )
        m_ref[here, :] = m_new


def iota(shape, dim):
    return lax.broadcasted_iota(jnp.int32, shape, dim)


def finish(acc):
    return (acc[:, :HEAD_DIM] / acc[:, HEAD_DIM:]).astype(jnp.bfloat16)


def stage_kernel(first, last, with_decode, pre_rows, heads, row_dev, info, *refs):
    refs = list(refs)
    own_ref, oth_ref, q_ref = refs[:3]
    refs = refs[3:]
    if not first:
        m_in, acc_in = refs[:2]
        refs = refs[2:]
    if with_decode:
        dq_ref = refs.pop(0)
        if first:
            nk_ref, nv_ref = refs[:2]
            refs = refs[2:]
        else:
            dm_in, dacc_in = refs[:2]
            refs = refs[2:]
    if last:
        o_ref = refs.pop(0)
        if with_decode:
            do_ref = refs.pop(0)
    else:
        m_out, acc_out = refs[:2]
        refs = refs[2:]
        if with_decode:
            dm_out, dacc_out = refs[:2]
            refs = refs[2:]
    k2, v2, m_ref, acc_ref = refs
    length, source, q_index, side = info[0], info[1], info[2], info[3]
    parts, total, _ = own_ref.shape
    chk_rows = total - pre_rows
    pre_all, chk_all = parts * pre_rows, parts * chk_rows
    pre_part, chk_part = pl.ds(0, pre_all), pl.ds(pre_all, chk_all)
    step = pl.program_id(0)

    def place(key_ref, value_ref):
        for part in range(parts):
            spots = (pl.ds(part * pre_rows, pre_rows), pl.ds(pre_all + part * chk_rows, chk_rows))
            froms = (pl.ds(0, pre_rows), pl.ds(pre_rows, chk_rows))
            for spot, source_rows in zip(spots, froms):
                k2[spot, :] = key_ref[part, source_rows, :]
                v2[spot, pl.ds(0, HEAD_DIM)] = value_ref[part, source_rows, :]

    @pl.when(step == 0)
    def _():
        v2[:, HEAD_DIM:] = jnp.ones((v2.shape[0], HEAD_DIM), jnp.bfloat16)

        @pl.when(side == 0)
        def _():
            place(own_ref, oth_ref)

        @pl.when(side != 0)
        def _():
            place(oth_ref, own_ref)

    live = length - source * pre_all

    def fold_prefix(q_of, rows):
        @pl.when(live >= pre_all)
        def _():
            fold(q_of, rows, k2[pre_part, :], v2[pre_part, :], m_ref, acc_ref)

        @pl.when((live > 0) & (live < pre_all))
        def _():
            fold(
                q_of,
                rows,
                k2[pre_part, :],
                v2[pre_part, :],
                m_ref,
                acc_ref,
                lambda start, shape: iota(shape, 1) < live,
            )

    if with_decode:

        @pl.when(step == 0)
        def _():
            share = dq_ref.shape[0]
            state = pl.ds(0, share)
            dq_of = lambda start, size: dq_ref[pl.ds(start, size), :]
            if first:
                m_ref[state, :] = jnp.full((share, HEAD_DIM), LOW, jnp.float32)
                acc_ref[state, :] = jnp.zeros((share, 2 * HEAD_DIM), jnp.float32)
                fresh = nk_ref.shape[0]
                nv2 = jnp.concatenate(
                    [nv_ref[...], jnp.ones((fresh, HEAD_DIM), jnp.bfloat16)], axis=1
                )

                def own(start, shape):
                    row = info[4] * share + start + iota(shape, 0)
                    col = iota(shape, 1)
                    return ((row // heads) % row_dev == col % row_dev) & (
                        col // row_dev <= row // (heads * row_dev)
                    )

                fold(dq_of, share, nk_ref[...], nv2, m_ref, acc_ref, own)
            else:
                m_ref[state, :] = dm_in[...]
                acc_ref[state, :] = dacc_in[...]
            fold(dq_of, share, k2[chk_part, :], v2[chk_part, :], m_ref, acc_ref)
            fold_prefix(dq_of, share)
            if last:
                do_ref[...] = finish(acc_ref[state, :])
            else:
                dm_out[...] = m_ref[state, :]
                dacc_out[...] = acc_ref[state, :]

    q_rows = q_ref.shape[1]
    q_of = lambda start, size: q_ref[0, pl.ds(start, size), :]
    if first:
        m_ref[...] = jnp.full_like(m_ref, LOW)
        acc_ref[...] = jnp.zeros_like(acc_ref)
    else:
        m_ref[...] = m_in[...]
        acc_ref[...] = acc_in[...]
    q_start = q_index * q_rows
    chk_base = source * chk_all

    @pl.when(chk_base + chk_all <= q_start + 1)
    def _():
        fold(q_of, q_rows, k2[chk_part, :], v2[chk_part, :], m_ref, acc_ref)

    @pl.when((chk_base + chk_all > q_start + 1) & (chk_base < q_start + q_rows))
    def _():
        fold(
            q_of,
            q_rows,
            k2[chk_part, :],
            v2[chk_part, :],
            m_ref,
            acc_ref,
            lambda start, shape: chk_base + iota(shape, 1) <= q_start + start + iota(shape, 0),
        )

    fold_prefix(q_of, q_rows)
    if last:
        o_ref[0] = finish(acc_ref[...])
    else:
        m_out[...] = m_ref[...]
        acc_out[...] = acc_ref[...]


def stage(info, own, oth, q, state, dec, first, last, pre_rows, heads_all, row_dev):
    _, q_rows, width = q.shape
    heads = width // HEAD_DIM
    parts, total, _ = own.shape
    keys = parts * total
    fixed3 = pl.BlockSpec(own.shape, lambda h, info: (0, 0, 0), pipeline_mode=pl.Buffered(1))
    q_spec = pl.BlockSpec((1, q_rows, HEAD_DIM), lambda h, info: (0, 0, h))
    state_specs = [
        pl.BlockSpec((q_rows, HEAD_DIM), lambda h, info: (0, h)),
        pl.BlockSpec((q_rows, 2 * HEAD_DIM), lambda h, info: (0, h)),
    ]

    def fixed(x):
        return pl.BlockSpec(x.shape, lambda h, info: (0, 0), pipeline_mode=pl.Buffered(1))

    args, in_specs = [own, oth, q], [fixed3, fixed3, q_spec]
    if not first:
        args += list(state)
        in_specs += state_specs
    if dec is not None:
        args += list(dec)
        in_specs += [fixed(x) for x in dec]
    if last:
        outs, out_specs = [jax.ShapeDtypeStruct(q.shape, jnp.bfloat16)], [q_spec]
    else:
        outs = [
            jax.ShapeDtypeStruct((q_rows, width), jnp.float32),
            jax.ShapeDtypeStruct((q_rows, 2 * width), jnp.float32),
        ]
        out_specs = list(state_specs)
    if dec is not None:
        share = dec[0].shape[0]
        if last:
            more = [jax.ShapeDtypeStruct((share, HEAD_DIM), jnp.bfloat16)]
        else:
            more = [
                jax.ShapeDtypeStruct((share, HEAD_DIM), jnp.float32),
                jax.ShapeDtypeStruct((share, 2 * HEAD_DIM), jnp.float32),
            ]
        outs += more
        out_specs += [pl.BlockSpec(x.shape, lambda h, info: (0, 0)) for x in more]
    rows = q_rows * heads
    return pl.pallas_call(
        functools.partial(
            stage_kernel, first, last, dec is not None, pre_rows, heads_all, row_dev
        ),
        out_shape=outs,
        grid_spec=pltpu.PrefetchScalarGridSpec(
            num_scalar_prefetch=1,
            grid=(heads,),
            in_specs=in_specs,
            out_specs=out_specs,
            scratch_shapes=[
                pltpu.VMEM((keys, HEAD_DIM), jnp.bfloat16),
                pltpu.VMEM((keys, 2 * HEAD_DIM), jnp.bfloat16),
                pltpu.VMEM((q_rows, HEAD_DIM), jnp.float32),
                pltpu.VMEM((q_rows, 2 * HEAD_DIM), jnp.float32),
            ],
        ),
        compiler_params=pltpu.CompilerParams(
            dimension_semantics=("arbitrary",), vmem_limit_bytes=56 * 2**20
        ),
        cost_estimate=pl.CostEstimate(
            flops=rows * keys * HEAD_DIM * 12, transcendentals=rows * keys, bytes_accessed=rows * 2048
        ),
        name="stage",
    )(info, *args)


def shifted(x, axis, shift):
    count = lax.axis_size(axis)
    return lax.ppermute(x, axis, [(i, (i + shift) % count) for i in range(count)])


def local(
    queries,
    prefix_keys,
    prefix_values,
    stretch_keys,
    stretch_values,
    prefix_lengths,
    decode_queries,
    new_keys,
    new_values,
    row_prompts,
):
    prompts, q_rows, width = queries.shape
    sides, blks = lax.axis_size("head"), lax.axis_size("blk")
    assert prompts == sides and lax.axis_size("rep") == 2
    x, z, core = lax.axis_index("head"), lax.axis_index("blk"), lax.axis_index("rep")
    pre_rows = prefix_keys.shape[1]

    def pick(array, index):
        return lax.dynamic_index_in_dim(array, index % prompts, keepdims=True)

    mine = jnp.concatenate(
        [
            jnp.where(core == 0, prefix_keys, prefix_values),
            jnp.where(core == 0, stretch_keys, stretch_values),
        ],
        axis=1,
    )
    pieces = [pick(mine, x)] + [shifted(pick(mine, x + s), "head", s) for s in range(1, sides)]
    held = jnp.zeros((sides,) + mine.shape[1:], mine.dtype)
    for s in range(sides):
        held = lax.dynamic_update_slice_in_dim(held, pieces[s], (x - s) % sides, 0)
    q_groups = [pick(queries, x)] + [
        shifted(pick(queries, x + s), "head", s) for s in range(1, sides)
    ]
    length = lax.dynamic_index_in_dim(prefix_lengths, x, keepdims=False)

    steps, row_dev, decode_width = decode_queries.shape
    heads_all = decode_width // HEAD_DIM
    rows_all = steps * row_dev * heads_all
    share = rows_all // blks
    dq = lax.dynamic_slice_in_dim(
        decode_queries.reshape(rows_all, HEAD_DIM), z * share, share, 0
    )
    nk, nv = new_keys.reshape(-1, HEAD_DIM), new_values.reshape(-1, HEAD_DIM)

    states = [None] * sides
    dec_state = None
    outs = [None] * sides
    q_index = lax.axis_index(("blk", "rep"))
    for turn in range(blks):
        first, last = turn == 0, turn == blks - 1
        coming = None if last else shifted(held, "blk", 1)
        other = shifted(held, "rep", 1)
        info = jnp.stack([length, (z - turn) % blks, q_index, core, z]).astype(jnp.int32)
        order = list(range(sides))
        if last:
            order = order[1:] + order[:1]
        for spot, s in enumerate(order):
            dec = None
            if s == 0:
                dec = (dq, nk, nv) if first else (dq, *dec_state)
            result = stage(
                info, held, other, q_groups[s], states[s], dec, first, last,
                pre_rows, heads_all, row_dev,
            )
            if last:
                outs[s] = result[0]
                if s == 0:
                    dec_out = result[1]
            else:
                states[s] = result[:2]
                if s == 0:
                    dec_state = result[2:]
                if first and s + 1 < sides:
                    q_groups[s + 1], states[s] = lax.optimization_barrier((q_groups[s + 1], states[s]))
                if spot == (sides - 1 if first else 0):
                    coming, states[s] = lax.optimization_barrier((coming, states[s]))
        held = coming

    backs = [outs[0]] + [shifted(outs[s], "head", -s) for s in range(1, sides)]
    prefill_out = jnp.zeros(queries.shape, queries.dtype)
    for s in range(sides):
        prefill_out = lax.dynamic_update_slice_in_dim(prefill_out, backs[s], (x + s) % sides, 0)

    flat = jnp.broadcast_to(row_prompts[None, :, None], (steps, row_dev, heads_all)).reshape(-1, 1)
    wanted = lax.dynamic_slice_in_dim(flat, z * share, share, 0)
    chosen = dec_out
    for s in range(1, sides):
        chosen = jnp.where(wanted == (x - s) % sides, shifted(dec_out, "head", s), chosen)
    decode_all = jnp.zeros((rows_all, HEAD_DIM), jnp.bfloat16)
    for s in range(blks):
        block = chosen if s == 0 else shifted(chosen, "blk", s)
        decode_all = lax.dynamic_update_slice_in_dim(decode_all, block, ((z - s) % blks) * share, 0)
    return (prefill_out, decode_all.reshape(decode_queries.shape))


def solution(mesh):
    placed = (
        P("groups", ("blk", "rep"), "head"),
        P("groups", ("blk", "head"), None),
        P("groups", ("blk", "head"), None),
        P("groups", ("blk", "head"), None),
        P("groups", ("blk", "head"), None),
        P("groups"),
        P("groups", "rep", None),
        P("groups", "rep", None),
        P("groups", "rep", None),
        P(("groups", "rep")),
    )
    return jax.shard_map(
        local,
        mesh=mesh,
        in_specs=placed,
        out_specs=(P("groups", ("blk", "rep"), "head"), P("groups", "rep", None)),
        check_vma=False,
    )
```

```python
import functools

import jax
import jax.numpy as jnp
from jax import lax
from jax.experimental import pallas as pl
from jax.experimental.pallas import tpu as pltpu
from jax.sharding import PartitionSpec as P

HEAD_DIM = 128
SCALE_LOG2E = HEAD_DIM ** (-0.5) * 1.4426950408889634
LOW = -1e30
CHAIN = 128
UNIT = 128


def fold(q_of, rows, k, v2, m_ref, acc_ref, seen=None):
    chain = min(CHAIN, rows)
    scores = []
    for start in range(0, rows, chain):
        s = lax.dot_general(
            q_of(start, chain), k, (((1,), (1,)), ((), ())), preferred_element_type=jnp.float32
        )
        if seen is not None:
            s = jnp.where(seen(start, s.shape), s, LOW)
        scores.append(s)
    for index, start in enumerate(range(0, rows, chain)):
        s = scores[index]
        here = pl.ds(start, chain)
        m_prev = m_ref[here, :]
        m_new = jnp.maximum(m_prev, jnp.max(s, axis=-1, keepdims=True))
        p = jnp.exp2(s * SCALE_LOG2E - (m_new * SCALE_LOG2E)[:, :1]).astype(jnp.bfloat16)
        alpha = jnp.exp2((m_prev - m_new) * SCALE_LOG2E)
        alpha2 = jnp.concatenate([alpha, alpha], axis=1)
        acc_ref[here, :] = acc_ref[here, :] * alpha2 + jnp.dot(
            p, v2, preferred_element_type=jnp.float32
        )
        m_ref[here, :] = m_new


def iota(shape, dim):
    return lax.broadcasted_iota(jnp.int32, shape, dim)


def finish(acc):
    return (acc[:, :HEAD_DIM] / acc[:, HEAD_DIM:]).astype(jnp.bfloat16)


def stage_kernel(turn, blks, last, with_decode, joined, pre_rows, heads, row_dev, info, *refs):
    first = turn == 0
    refs = list(refs)
    own_ref, oth_ref, q_ref = refs[:3]
    refs = refs[3:]
    if not first:
        m_in, acc_in = refs[:2]
        refs = refs[2:]
    elif joined:
        refs = refs[2:]
    if with_decode:
        dq_ref = refs.pop(0)
        if first:
            nk_ref, nv_ref = refs[:2]
        else:
            dm_in, dacc_in = refs[:2]
        refs = refs[2:]
    if last:
        o_ref = refs.pop(0)
        if with_decode:
            do_ref = refs.pop(0)
    else:
        m_out, acc_out = refs[:2]
        refs = refs[2:]
        if with_decode:
            dm_out, dacc_out = refs[:2]
            refs = refs[2:]
    k2, v2, m_ref, acc_ref = refs
    length, z, q_index, side = info[0], info[1], info[2], info[3]
    source = lax.rem(z + (blks - turn), blks)
    parts, total, _ = own_ref.shape
    chk_rows = total - pre_rows
    pre_all, chk_all = parts * pre_rows, parts * chk_rows
    everything = pl.ds(0, pre_all + chk_all)
    pre_part, chk_part = pl.ds(0, pre_all), pl.ds(pre_all, chk_all)
    step = pl.program_id(0)
    live = jnp.clip(length - source * pre_all, 0, pre_all)
    lowest = jnp.where(live > 0, 0, pre_all)

    def place(key_ref, value_ref):
        for part in range(parts):
            spots = (pl.ds(part * pre_rows, pre_rows), pl.ds(pre_all + part * chk_rows, chk_rows))
            froms = (pl.ds(0, pre_rows), pl.ds(pre_rows, chk_rows))
            for spot, source_rows in zip(spots, froms):
                k2[spot, :] = key_ref[part, source_rows, :]
                v2[spot, pl.ds(0, HEAD_DIM)] = value_ref[part, source_rows, :]

    @pl.when(step == 0)
    def _():
        v2[:, HEAD_DIM:] = jnp.ones((v2.shape[0], HEAD_DIM), jnp.bfloat16)

        @pl.when(side == 0)
        def _():
            place(own_ref, oth_ref)

        @pl.when(side != 0)
        def _():
            place(oth_ref, own_ref)

        @pl.when(live > 0)
        def _():
            @pl.loop(live // UNIT, pre_all // UNIT)
            def _(i):
                spot = pl.ds(pl.multiple_of(i * UNIT, UNIT), UNIT)
                k2[spot, :] = k2[pl.ds(0, UNIT), :]
                v2[spot, :] = jnp.zeros((UNIT, 2 * HEAD_DIM), jnp.bfloat16)

    def run(q_of, rows, part, seen=None):
        fold(q_of, rows, k2[part, :], v2[part, :], m_ref, acc_ref, seen)

    if with_decode:

        @pl.when(step == 0)
        def _():
            share = dq_ref.shape[0]
            state = pl.ds(0, share)
            dq_of = lambda start, size: dq_ref[pl.ds(start, size), :]
            if first:
                m_ref[state, :] = jnp.full((share, HEAD_DIM), LOW, jnp.float32)
                acc_ref[state, :] = jnp.zeros((share, 2 * HEAD_DIM), jnp.float32)
                fresh = nk_ref.shape[0]
                nv2 = jnp.concatenate(
                    [nv_ref[...], jnp.ones((fresh, HEAD_DIM), jnp.bfloat16)], axis=1
                )

                def own(start, shape):
                    row = z * share + start + iota(shape, 0)
                    col = iota(shape, 1)
                    return ((row // heads) % row_dev == col % row_dev) & (
                        col // row_dev <= row // (heads * row_dev)
                    )

                fold(dq_of, share, nk_ref[...], nv2, m_ref, acc_ref, own)
                run(dq_of, share, everything, lambda start, shape: iota(shape, 1) >= lowest)
            else:
                m_ref[state, :] = dm_in[...]
                acc_ref[state, :] = dacc_in[...]

                @pl.when(live > 0)
                def _():
                    run(dq_of, share, everything)

                @pl.when(live == 0)
                def _():
                    run(dq_of, share, chk_part)

            if last:
                do_ref[...] = finish(acc_ref[state, :])
            else:
                dm_out[...] = m_ref[state, :]
                dacc_out[...] = acc_ref[state, :]

    q_rows = q_ref.shape[1]
    q_of = lambda start, size: q_ref[0, pl.ds(start, size), :]
    ahead = q_index * q_rows - source * chk_all
    if first:
        m_ref[...] = jnp.full_like(m_ref, LOW)
        acc_ref[...] = jnp.zeros_like(acc_ref)

        def seen(start, shape):
            col = iota(shape, 1)
            return (col - pre_all <= ahead + start + iota(shape, 0)) & (col >= lowest)

        run(q_of, q_rows, everything, seen)
    else:
        m_ref[...] = m_in[...]
        acc_ref[...] = acc_in[...]

        @pl.when((live > 0) & (ahead > 0))
        def _():
            run(q_of, q_rows, everything)

        @pl.when((live > 0) & (ahead <= 0))
        def _():
            run(q_of, q_rows, pre_part)

        @pl.when((live == 0) & (ahead > 0))
        def _():
            run(q_of, q_rows, chk_part)

    if last:
        o_ref[0] = finish(acc_ref[...])
    else:
        m_out[...] = m_ref[...]
        acc_out[...] = acc_ref[...]


def stage(info, own, oth, q, state, dec, turn, blks, offset, heads_all, pre_rows, dec_heads, row_dev):
    first, last = turn == 0, turn == blks - 1
    _, q_rows, width = q.shape
    heads = width // HEAD_DIM
    parts, total, _ = own.shape
    keys = parts * total
    fixed3 = pl.BlockSpec(own.shape, lambda h, info: (0, 0, 0), pipeline_mode=pl.Buffered(1))
    q_spec = pl.BlockSpec((1, q_rows, HEAD_DIM), lambda h, info: (0, 0, h))
    state_specs = [
        pl.BlockSpec((q_rows, HEAD_DIM), lambda h, info: (0, h + offset)),
        pl.BlockSpec((q_rows, 2 * HEAD_DIM), lambda h, info: (0, h + offset)),
    ]

    def fixed(x):
        return pl.BlockSpec(x.shape, lambda h, info: (0, 0), pipeline_mode=pl.Buffered(1))

    args, in_specs, aliases = [own, oth, q], [fixed3, fixed3, q_spec], {}
    if state is not None:
        args += list(state)
        in_specs += [pl.BlockSpec(memory_space=pl.ANY)] * 2 if first else state_specs
        if first:
            aliases = {4: 0, 5: 1}
    if dec is not None:
        args += list(dec)
        in_specs += [fixed(x) for x in dec]
    if last:
        outs, out_specs = [jax.ShapeDtypeStruct(q.shape, jnp.bfloat16)], [q_spec]
    else:
        outs = [
            jax.ShapeDtypeStruct((q_rows, heads_all * HEAD_DIM), jnp.float32),
            jax.ShapeDtypeStruct((q_rows, heads_all * 2 * HEAD_DIM), jnp.float32),
        ]
        out_specs = list(state_specs)
    if dec is not None:
        share = dec[0].shape[0]
        if last:
            more = [jax.ShapeDtypeStruct((share, HEAD_DIM), jnp.bfloat16)]
        else:
            more = [
                jax.ShapeDtypeStruct((share, HEAD_DIM), jnp.float32),
                jax.ShapeDtypeStruct((share, 2 * HEAD_DIM), jnp.float32),
            ]
        outs += more
        out_specs += [pl.BlockSpec(x.shape, lambda h, info: (0, 0)) for x in more]
    rows = q_rows * heads
    return pl.pallas_call(
        functools.partial(
            stage_kernel, turn, blks, last, dec is not None, state is not None, pre_rows, dec_heads, row_dev
        ),
        out_shape=outs,
        grid_spec=pltpu.PrefetchScalarGridSpec(
            num_scalar_prefetch=1,
            grid=(heads,),
            in_specs=in_specs,
            out_specs=out_specs,
            scratch_shapes=[
                pltpu.VMEM((keys, HEAD_DIM), jnp.bfloat16),
                pltpu.VMEM((keys, 2 * HEAD_DIM), jnp.bfloat16),
                pltpu.VMEM((q_rows, HEAD_DIM), jnp.float32),
                pltpu.VMEM((q_rows, 2 * HEAD_DIM), jnp.float32),
            ],
        ),
        compiler_params=pltpu.CompilerParams(
            dimension_semantics=("arbitrary",), vmem_limit_bytes=56 * 2**20
        ),
        cost_estimate=pl.CostEstimate(
            flops=rows * keys * HEAD_DIM * 12, transcendentals=rows * keys, bytes_accessed=rows * 2048
        ),
        input_output_aliases=aliases,
        name="stage",
    )(info, *args)


def shifted(x, axis, shift):
    count = lax.axis_size(axis)
    return lax.ppermute(x, axis, [(i, (i + shift) % count) for i in range(count)])


def local(
    queries,
    prefix_keys,
    prefix_values,
    stretch_keys,
    stretch_values,
    prefix_lengths,
    decode_queries,
    new_keys,
    new_values,
    row_prompts,
):
    prompts, q_rows, width = queries.shape
    sides, blks = lax.axis_size("head"), lax.axis_size("blk")
    assert prompts == sides and lax.axis_size("rep") == 2
    x, z, core = lax.axis_index("head"), lax.axis_index("blk"), lax.axis_index("rep")
    pre_rows = prefix_keys.shape[1]

    def pick(array, index):
        return lax.dynamic_index_in_dim(array, index % prompts, keepdims=True)

    mine = jnp.concatenate(
        [
            jnp.where(core == 0, prefix_keys, prefix_values),
            jnp.where(core == 0, stretch_keys, stretch_values),
        ],
        axis=1,
    )
    pieces = [pick(mine, x)] + [shifted(pick(mine, x + s), "head", s) for s in range(1, sides)]
    held = jnp.zeros((sides,) + mine.shape[1:], mine.dtype)
    for s in range(sides):
        held = lax.dynamic_update_slice_in_dim(held, pieces[s], (x - s) % sides, 0)
    q_groups = [pick(queries, x)] + [
        shifted(pick(queries, x + s), "head", s) for s in range(1, sides)
    ]
    length = lax.dynamic_index_in_dim(prefix_lengths, x, keepdims=False)

    steps, row_dev, decode_width = decode_queries.shape
    heads_all = decode_width // HEAD_DIM
    rows_all = steps * row_dev * heads_all
    share = rows_all // blks
    dq = lax.dynamic_slice_in_dim(
        decode_queries.reshape(rows_all, HEAD_DIM), z * share, share, 0
    )
    nk, nv = new_keys.reshape(-1, HEAD_DIM), new_values.reshape(-1, HEAD_DIM)

    heads_total = sides * width // HEAD_DIM
    group_heads = width // HEAD_DIM
    assert blks > 1 and pre_rows % UNIT == 0
    info = jnp.stack([length, z, lax.axis_index(("blk", "rep")), core]).astype(jnp.int32)
    fixed = (heads_total, pre_rows, heads_all, row_dev)
    outs = [None] * sides
    state = None
    for turn in range(blks):
        first, last = turn == 0, turn == blks - 1
        coming = None if last else shifted(held, "blk", 1)
        other = shifted(held, "rep", 1)
        if first:
            for s in range(sides):
                dec = (dq, nk, nv) if s == 0 else None
                result = stage(
                    info, held, other, q_groups[s], state, dec, turn, blks, s * group_heads, *fixed
                )
                state = tuple(result[:2])
                if s == 0:
                    dec_state = result[2:]
                if s + 1 < sides:
                    q_groups[s + 1], state = lax.optimization_barrier((q_groups[s + 1], state))
            coming, state = lax.optimization_barrier((coming, state))
            q_all = jnp.concatenate(q_groups, axis=2)
        elif not last:
            result = stage(
                info, held, other, q_all, state, (dq, *dec_state), turn, blks, 0, *fixed
            )
            state, dec_state = tuple(result[:2]), result[2:]
            coming, state = lax.optimization_barrier((coming, state))
        else:
            for s in list(range(1, sides)) + [0]:
                dec = (dq, *dec_state) if s == min(1, sides - 1) else None
                result = stage(
                    info, held, other, q_groups[s], state, dec, turn, blks, s * group_heads, *fixed
                )
                outs[s] = result[0]
                if dec is not None:
                    dec_out = result[1]
                if s != 0:
                    outs[s], state = lax.optimization_barrier((outs[s], state))
        held = coming

    backs = [outs[0]] + [shifted(outs[s], "head", -s) for s in range(1, sides)]
    prefill_out = jnp.zeros(queries.shape, queries.dtype)
    for s in range(sides):
        prefill_out = lax.dynamic_update_slice_in_dim(prefill_out, backs[s], (x + s) % sides, 0)

    flat = jnp.broadcast_to(row_prompts[None, :, None], (steps, row_dev, heads_all)).reshape(-1, 1)
    wanted = lax.dynamic_slice_in_dim(flat, z * share, share, 0)
    chosen = dec_out
    for s in range(1, sides):
        chosen = jnp.where(wanted == (x - s) % sides, shifted(dec_out, "head", s), chosen)
    decode_all = jnp.zeros((rows_all, HEAD_DIM), jnp.bfloat16)
    for s in range(blks):
        block = chosen if s == 0 else shifted(chosen, "blk", s)
        decode_all = lax.dynamic_update_slice_in_dim(decode_all, block, ((z - s) % blks) * share, 0)
    return (prefill_out, decode_all.reshape(decode_queries.shape))


def solution(mesh):
    placed = (
        P("groups", ("blk", "rep"), "head"),
        P("groups", ("blk", "head"), None),
        P("groups", ("blk", "head"), None),
        P("groups", ("blk", "head"), None),
        P("groups", ("blk", "head"), None),
        P("groups"),
        P("groups", "rep", None),
        P("groups", "rep", None),
        P("groups", "rep", None),
        P(("groups", "rep")),
    )
    return jax.shard_map(
        local,
        mesh=mesh,
        in_specs=placed,
        out_specs=(P("groups", ("blk", "rep"), "head"), P("groups", "rep", None)),
        check_vma=False,
    )
```
